32 devices in a mesh: grp: 2 (over x), win: 4 (over z), seq: 4 (over y, core).
Axes of the slice: x: 2, y: 2, z: 4, core: 2. Of those that a mesh axis runs over, the one named last changes fastest.
Arguments:
- embeddings: bfloat16 [8, 768, 1536], P(('grp', 'win'), 'seq'), parts along dimension 0, may hold values from -48 to 48
- skip_rows: bfloat16 [8, 1536, 1536], P(('grp', 'win'), 'seq'), parts along dimension 0, may hold values from -6 to 6
- w_query: bfloat16 [1536, 256], replicated, may hold values from -0.16 to 0.16
- w_key: bfloat16 [1536, 256], replicated, may hold values from -10 to 10
- w_value: bfloat16 [1536, 768], replicated, may hold values from -0.15625 to 0.15625
- w_out: bfloat16 [768, 1536], replicated, may hold values from -0.21875 to 0.21875
- conv_taps: float32 [3, 1536], replicated, may hold values from -3 to 3
- w_head: bfloat16 [1536, 4096], P(None, 'seq'), may hold values from -0.15625 to 0.15625
- head_bias: float32 [4096], replicated, may hold values from -4 to 4
Outputs:
- genome_tracks: bfloat16 [8, 2, 4, 96, 4096], P(('grp', 'win'), None, 'seq'), parts along dimension 0
The draws below stay inside these ranges and needn't reach their ends.
There are 2 independent parts, one for each index of `grp`. The reference program is written for one: setup_inputs(seed, part) draws one part's arguments, and reference() takes and returns one part's arrays. A program takes and returns all parts, laid end to end along the dimension named above; an argument that names none is the same for every part. Nothing has to cross between parts.
All inputs are finite; a program needn't handle non-finite values.
Results may differ from the reference program's by a relative error of at most 0.0075.
Values may be sent and summed in bfloat16 or wider, within the bound.
A program may use at most 128 MiB of HBM per device.

```python
import math
import jax
import jax.numpy as jnp
from jax import lax

D = 1536
HEADS = 4
KEY = 64
VAL = 192
TRACKS = 4096
WIN_LEN = 768
PIECE = 96
N_WIN = 4
N_SEQ = 4


def draw_pair(key):
    limit = min(6.0 / math.sqrt(D), 0.155)
    first = jax.random.normal(jax.random.fold_in(key, 11), (D, HEADS * KEY), jnp.float32) / math.sqrt(D)
    second = jax.random.normal(jax.random.fold_in(key, 12), (D, HEADS * KEY), jnp.float32) / math.sqrt(D)
    first = jnp.clip(first, -limit, limit)
    second = 4.0 * jnp.clip(second, -limit, limit)
    return (first, second)


def draw_w_query(key, part):
    return draw_pair(key)[0].astype(jnp.bfloat16)


def draw_w_key(key, part):
    return draw_pair(key)[1].astype(jnp.bfloat16)


def draw_embeddings(key, part):
    base = jax.random.normal(jax.random.fold_in(key, 21), (N_WIN, WIN_LEN, D), jnp.float32)
    base = jnp.clip(base, -6.0, 6.0)
    return base.astype(jnp.bfloat16)


def steps_of(rng, extent, shards, low, top_value):
    level = 1.0
    for axis_at, blocks in shards:
        steps = jax.random.uniform(jax.random.fold_in(jax.random.fold_in(rng, 6), axis_at), (blocks,), jnp.float32, low / len(shards), top_value / len(shards))
        level = level * jnp.repeat(jnp.exp(steps), extent[axis_at] // blocks).reshape((-1,) + (1,) * (len(extent) - 1 - axis_at))
    return level


def bell_draw(rng, dims, width, reach, pieces=(), kind=jnp.bfloat16):
    values = jax.random.normal(rng, dims, jnp.float32) * width
    if len(pieces) > 0:
        values = steps_of(rng, dims, pieces, -0.22, 0.18) * values
    return jnp.clip(values, min=-reach, max=reach).astype(kind)


def setup_inputs(seed: int = 0, part: int = 0) -> dict:
    key_list = jax.random.split(jax.random.key(seed), 10)
    own_keys = jax.random.split(jax.random.fold_in(key_list[9], part), 10)
    return {
        "embeddings": draw_embeddings(jax.random.fold_in(jax.random.fold_in(key_list[9], part), 71), part),
        "skip_rows": bell_draw(own_keys[1], (N_WIN, 2 * WIN_LEN, D), 1.0, 6.0, ((0, 4), (1, 4))),
        "w_query": draw_w_query(jax.random.fold_in(key_list[9], 71), part),
        "w_key": draw_w_key(jax.random.fold_in(key_list[9], 71), part),
        "w_value": bell_draw(key_list[4], (D, HEADS * VAL), D ** -0.5, 0.15625),
        "w_out": bell_draw(key_list[5], (HEADS * VAL, D), (HEADS * VAL) ** -0.5, 0.21875),
        "conv_taps": bell_draw(key_list[6], (3, D), 0.6, 3.0, (), jnp.float32),
        "w_head": bell_draw(key_list[7], (D, TRACKS), D ** -0.5, 0.15625, ((1, 4),)),
        "head_bias": bell_draw(key_list[8], (TRACKS,), 1.0, 4.0, (), jnp.float32),
    }


def rounded(values):
    return lax.optimization_barrier(values.astype(jnp.bfloat16))

def normalize(rows):
    centre = lax.optimization_barrier(jnp.mean(rows, axis=-1, keepdims=True))
    centred = rows - centre
    spread = lax.optimization_barrier(jnp.mean(centred * centred, axis=-1, keepdims=True))
    return centred * lax.rsqrt(spread + 1e-05)

def reference(embeddings, skip_rows, w_query, w_key, w_value, w_out, conv_taps, w_head, head_bias):

    def window_tracks(pair):
        embed_win, skip_win = pair
        length = embed_win.shape[0]
        x_float = embed_win.astype(jnp.float32)
        normed = normalize(x_float).astype(jnp.bfloat16)
        query = rounded(jnp.dot(normed, w_query, preferred_element_type=jnp.float32)).reshape(length, HEADS, KEY)
        key_rows = rounded(jnp.dot(normed, w_key, preferred_element_type=jnp.float32)).reshape(length, HEADS, KEY)
        value_rows = rounded(jnp.dot(normed, w_value, preferred_element_type=jnp.float32)).reshape(length, HEADS, VAL)
        scores = jnp.einsum('thk,nhk->thn', query.astype(jnp.float32), key_rows.astype(jnp.float32)) / math.sqrt(KEY)
        top_score = lax.optimization_barrier(jnp.max(scores, axis=-1, keepdims=True))
        expo = jnp.exp(scores - top_score)
        denom_sum = lax.optimization_barrier(jnp.sum(expo, axis=-1))
        weights = rounded(expo).astype(jnp.float32)
        attended = jnp.einsum('thn,nhv->thv', weights, value_rows.astype(jnp.float32)) / denom_sum[..., None]
        attended = attended.reshape(length, HEADS * VAL).astype(jnp.bfloat16)
        resid = x_float + jnp.dot(attended, w_out, preferred_element_type=jnp.float32)
        upsampled = rounded(jnp.repeat(resid, 2, axis=0) + skip_win.astype(jnp.float32)).astype(jnp.float32)
        padded = jnp.pad(upsampled, ((1, 1), (0, 0)))
        conv_out = conv_taps[0] * padded[:-2] + conv_taps[1] * padded[1:-1] + conv_taps[2] * padded[2:]
        features = jax.nn.gelu(conv_out, approximate=False).astype(jnp.bfloat16)
        return jnp.dot(features, w_head, preferred_element_type=jnp.float32).astype(jnp.bfloat16)
    tracks = lax.map(window_tracks, (embeddings, skip_rows))
    length = tracks.shape[1] // 2
    ahead_part = tracks[:, :length].astype(jnp.float32)
    behind = jnp.roll(tracks[:, length:], 1, axis=0).astype(jnp.float32)
    offsets = jnp.arange(length, dtype=jnp.int32).astype(jnp.float32)[:, None]
    stitched = ((offsets + 1.0) * ahead_part + (length - offsets) * behind) / (length + 1.0) + head_bias
    genome_tracks = jax.nn.softplus(stitched).astype(jnp.bfloat16)
    return genome_tracks.reshape(N_WIN, N_SEQ // 2, N_SEQ, PIECE, TRACKS)
```

```python
import functools
import math

import jax
import jax.numpy as jnp
from jax import lax
from jax.experimental import pallas as pl
from jax.experimental.pallas import tpu as pltpu
from jax.sharding import PartitionSpec as P

HEADS = 4
KEY = 64
VAL = 192
PAIRS = HEADS // 2
KP = 2 * KEY
VP = 2 * VAL
TILE = 256
MESH = pl.DeviceIdType.MESH


def normalize(rows):
    centre = jnp.mean(rows, axis=-1, keepdims=True)
    centred = rows - centre
    spread = jnp.mean(centred * centred, axis=-1, keepdims=True)
    return centred * lax.rsqrt(spread + 1e-05)


def gelu(x):
    return 0.5 * x * (1.0 + lax.erf(x * math.sqrt(0.5)))


def kernel(
    n, n_win, n_grp,
    emb_h, skip_h, wq_h, wk_h, wv_h, wo_h, taps_h, wh_h, bias_h, out_h,
    x_v, skip_v, wq_v, wk_v, wv_v, wo_v, taps_v, bias_v, wh_v,
    normed_v, q_v, kv_v, att_v, wide_v, even_v, odd_v, halo_s, halo_r,
    feat_v, got_v, blend_v, out_v,
    load_sem, send_sem, recv_sem, fsend_sem, frecv_sem, store_sem,
):
    grp = lax.axis_index("grp")
    win = lax.axis_index("win")
    seq = lax.axis_index("seq")
    tok, width = x_v.shape
    piece = feat_v.shape[1]
    cols = wh_v.shape[2]
    half = n // 2
    window_len = n * tok

    loads = {}
    for at, (name, src, dst) in enumerate(
        (
            ("x", emb_h.at[0], x_v),
            ("wk", wk_h, wk_v),
            ("wv", wv_h, wv_v),
            ("wq", wq_h, wq_v),
            ("skip", skip_h.at[0], skip_v),
            ("wo", wo_h, wo_v),
            ("taps", taps_h, taps_v),
            ("wh", wh_h, wh_v.at[seq]),
            ("bias", bias_h, bias_v),
        )
    ):
        loads[name] = pltpu.make_async_copy(src, dst, load_sem.at[at])
        loads[name].start()

    def dev(g, w, s):
        return (g, w, s)

    sibling = dev(grp, win, seq + 1 - 2 * (seq % 2))
    sib_seq = seq + 1 - 2 * (seq % 2)
    other_grp = 1 - grp
    other_win = win + 1 - 2 * (win % 2)
    across = dev(other_grp, win, seq)
    beside = dev(grp, other_win, seq)
    peers = [(seq + 2 * e) % n for e in range(1, half)]
    next_win = (win + 1) % n_win
    prev_win = (win + n_win - 1) % n_win

    barrier = pltpu.get_barrier_semaphore()
    greeted = [dev(grp, win, (seq + d) % n) for d in range(1, n)]
    greeted += [dev(grp, w, (seq + d) % n) for w in (next_win, prev_win) for d in range(n)]
    greeted.append(across)
    for target in greeted:
        pl.semaphore_signal(barrier, inc=1, device_id=target, device_id_type=MESH)
    pl.semaphore_wait(barrier, len(greeted))

    started = []

    def remote(src, dst, target):
        at = len(started)
        copy = pltpu.make_async_remote_copy(
            src_ref=src,
            dst_ref=dst,
            send_sem=send_sem.at[at],
            recv_sem=recv_sem.at[at],
            device_id=target,
            device_id_type=MESH,
        )
        copy.start()
        started.append(copy)
        return copy

    part = width // (2 * n_grp)
    chunk = part // 2

    def rows_of(g, w, c):
        return pl.ds(pl.multiple_of((g * 2 + w % 2) * part + c * chunk, chunk), chunk)

    def head_out(c):
        rows = rows_of(grp, win, c)
        return [remote(wh_h.at[rows], wh_v.at[seq, rows], dev(grp, win, p)) for p in peers]

    def head_spread(c, arrived):
        rows = rows_of(grp, win, c)
        by_x, by_z = [], []
        for e, copy in enumerate(arrived):
            copy.wait_recv()
            block = wh_v.at[(seq + n - 2 * (e + 1)) % n, rows]
            by_x.append(remote(block, block, across))
            by_z.append(remote(block, block, beside))
        return by_x, by_z

    def head_relay(c, by_x, by_z):
        relayed = []
        for e in range(half - 1):
            shard = (seq + n - 2 * (e + 1)) % n
            if c == 0:
                by_z[e].wait_recv()
                block = wh_v.at[shard, rows_of(grp, other_win, c)]
                relayed.append(remote(block, block, across))
            else:
                by_x[e].wait_recv()
                block = wh_v.at[shard, rows_of(other_grp, win, c)]
                relayed.append(remote(block, block, beside))
        return relayed

    arrive_0 = head_out(0)

    loads["x"].wait()
    normed_v[...] = normalize(x_v[...].astype(jnp.float32)).astype(jnp.bfloat16)
    loads["wk"].wait()
    loads["wv"].wait()
    kv_far, kv_near = [], []
    for p in range(PAIRS):
        kv_v[seq, p, :, :KP] = jnp.dot(
            normed_v[...], wk_v[:, p * KP : (p + 1) * KP], preferred_element_type=jnp.float32
        ).astype(jnp.bfloat16)
        kv_v[seq, p, :, KP:] = jnp.dot(
            normed_v[...], wv_v[:, p * VP : (p + 1) * VP], preferred_element_type=jnp.float32
        ).astype(jnp.bfloat16)
        block = kv_v.at[seq, p]
        kv_far.append([remote(block, block, dev(grp, win, s)) for s in peers])
        kv_near.append([remote(block, block, sibling)])
    arrive_1 = head_out(1)
    own_sib = remote(wh_h, wh_v.at[seq], sibling)
    loads["wq"].wait()
    q_v[...] = jnp.dot(normed_v[...], wq_v[...], preferred_element_type=jnp.float32).astype(
        jnp.bfloat16
    )
    loads["skip"].wait()
    for j in range(width // 128):
        wide_v[j] = skip_v[:, j * 128 : (j + 1) * 128].astype(jnp.float32)

    def kv_relay(p):
        for e in range(half - 1):
            kv_far[p][e].wait_recv()
            block = kv_v.at[(seq + n - 2 * (e + 1)) % n, p]
            kv_near[p].append(remote(block, block, sibling))

    def attend(p):
        for copy in kv_near[p]:
            copy.wait_recv()
        keys = kv_v[:, p, :, :KP].reshape(n * tok, KP)
        vals = kv_v[:, p, :, KP:].reshape(n * tok, VP)
        pair = q_v[:, p * KP : (p + 1) * KP]
        key_lane = lax.broadcasted_iota(jnp.int32, (tok, KP), 1)
        outs = []
        for h in range(2):
            mine = key_lane < KEY if h == 0 else key_lane >= KEY
            masked = jnp.where(mine, pair.astype(jnp.float32), 0.0).astype(jnp.bfloat16)
            scores = lax.dot_general(
                masked, keys, (((1,), (1,)), ((), ())), preferred_element_type=jnp.float32
            ) * (1.0 / math.sqrt(KEY))
            expo = jnp.exp(scores - jnp.max(scores, axis=-1, keepdims=True))
            denom = jnp.sum(expo, axis=-1, keepdims=True)
            outs.append(
                jnp.dot(expo.astype(jnp.bfloat16), vals, preferred_element_type=jnp.float32) / denom
            )
        val_lane = lax.broadcasted_iota(jnp.int32, (tok, VP), 1)
        att_v[:, p * VP : (p + 1) * VP] = jnp.where(val_lane < VAL, outs[0], outs[1]).astype(
            jnp.bfloat16
        )

    kv_relay(0)
    x_0, z_0 = head_spread(0, arrive_0)
    attend(0)
    for p in range(1, PAIRS):
        kv_relay(p)
        attend(p)
    relay_0 = head_relay(0, x_0, z_0)
    loads["wo"].wait()

    def up_step(t, carry):
        at = pl.ds(pl.multiple_of(t * TILE, TILE), TILE)
        resid = x_v[:, at].astype(jnp.float32) + jnp.dot(
            att_v[...], wo_v[:, at], preferred_element_type=jnp.float32
        )
        for m in range(2):
            here = pl.ds(pl.multiple_of(t * TILE + m * 128, 128), 128)
            mine = resid[:, m * 128 : (m + 1) * 128]
            even = (mine + wide_v[t * (TILE // 128) + m, pl.ds(0, tok, stride=2), :]).astype(jnp.bfloat16)
            odd = (mine + wide_v[t * (TILE // 128) + m, pl.ds(1, tok, stride=2), :]).astype(jnp.bfloat16)
            even = even.astype(jnp.float32)
            odd = odd.astype(jnp.float32)
            even_v[:, here] = even
            odd_v[:, here] = odd
            halo_s[0, :, here] = even[:8]
            halo_s[1, :, here] = odd[tok - 8 :]
        return carry

    lax.fori_loop(0, width // TILE, up_step, 0)
    to_prev = remote(halo_s.at[0], halo_r.at[0], dev(grp, win, (seq + n - 1) % n))
    to_next = remote(halo_s.at[1], halo_r.at[1], dev(grp, win, (seq + 1) % n))
    x_1, z_1 = head_spread(1, arrive_1)
    loads["taps"].wait()
    to_prev.wait_recv()
    to_next.wait_recv()

    def conv_step(t, carry):
        at = pl.ds(pl.multiple_of(t * 128, 128), 128)
        even = even_v[:, at]
        odd = odd_v[:, at]
        row = lax.broadcasted_iota(jnp.int32, (tok, 128), 0)
        before = jnp.where(seq == 0, 0.0, halo_r[1, 7:8, at])
        after = jnp.where(seq == n - 1, 0.0, halo_r[0, 0:1, at])
        odd_prev = jnp.where(row == 0, before, pltpu.roll(odd, 1, axis=0))
        even_next = jnp.where(row == tok - 1, after, pltpu.roll(even, tok - 1, axis=0))
        t0, t1, t2 = taps_v[0:1, at], taps_v[1:2, at], taps_v[2:3, at]
        first = t0 * odd_prev + t1 * even + t2 * odd
        second = t0 * even + t1 * odd + t2 * even_next
        wide_v[t, pl.ds(0, tok, stride=2), :] = gelu(first)
        wide_v[t, pl.ds(1, tok, stride=2), :] = gelu(second)
        return carry

    lax.fori_loop(0, width // 128, conv_step, 0)
    for k in range(n):
        for j in range(width // 128):
            feat_v[k, :, j * 128 : (j + 1) * 128] = wide_v[
                j, k * piece : (k + 1) * piece, :
            ].astype(jnp.bfloat16)

    ahead = seq // half
    to_win = (win + ahead) % n_win

    def feature_copy(d):
        owner = (seq + d) % n
        return pltpu.make_async_remote_copy(
            src_ref=feat_v.at[owner],
            dst_ref=got_v.at[seq],
            send_sem=fsend_sem.at[d],
            recv_sem=frecv_sem.at[d],
            device_id=dev(grp, to_win, owner),
            device_id_type=MESH,
        )

    feats = [feature_copy(d) for d in range(n)]
    for d in list(range(half, n)) + list(range(1, half)):
        feats[d].start()

    @pl.when(seq >= half)
    def _():
        feats[0].start()

    @pl.when(seq < half)
    def _():
        got_v[seq] = feat_v[seq]

    relay_1 = head_relay(1, x_1, z_1)
    late = []
    loads["wh"].wait()
    for e in range(half - 1):
        x_0[e].wait_recv()
        relay_0[e].wait_recv()
        z_1[e].wait_recv()
        relay_1[e].wait_recv()
        shard = wh_v.at[(seq + n - 2 * (e + 1)) % n]
        late.append(remote(shard, shard, sibling))
    loads["bias"].wait()

    for d in range(1, n):
        feats[d].wait_recv()

    @pl.when(seq >= half)
    def _():
        feats[0].wait_recv()

    def blend_step(t, carry):
        at = pl.ds(pl.multiple_of(t * 128, 128), 128)
        blocks = []
        for i in range(half):
            place = lax.broadcasted_iota(jnp.int32, (piece, 128), 0) + (i * n + seq) * piece
            place = place.astype(jnp.float32)
            blocks.append(
                (
                    (place + 1.0) * got_v[i, :, at].astype(jnp.float32)
                    + (window_len - place) * got_v[half + i, :, at].astype(jnp.float32)
                )
                * (1.0 / (window_len + 1.0))
            )
        blend_v[:, at] = jnp.concatenate(blocks, axis=0).astype(jnp.bfloat16)
        return carry

    lax.fori_loop(0, width // 128, blend_step, 0)

    def apply_head(shard):
        def head_step(t, carry):
            at = pl.ds(pl.multiple_of(t * TILE, TILE), TILE)
            base = pl.ds(pl.multiple_of(shard * cols + t * TILE, TILE), TILE)
            z = (
                jnp.dot(blend_v[...], wh_v[shard, :, at], preferred_element_type=jnp.float32)
                + bias_v[:, base]
            )
            z = jnp.maximum(z, 0.0) + jnp.log1p(jnp.exp(-jnp.abs(z)))
            for i in range(half):
                out_v[i, :, base] = z[i * piece : (i + 1) * piece].astype(jnp.bfloat16)
            return carry

        lax.fori_loop(0, cols // TILE, head_step, 0)

    stores = []

    def store(shard):
        base = pl.ds(pl.multiple_of(shard * cols, cols), cols)
        at = len(stores)
        stores.append(
            pltpu.make_async_copy(out_v.at[:, :, base], out_h.at[:, :, base], store_sem.at[at])
        )
        stores[at].start()

    apply_head(seq)
    store(seq)
    own_sib.wait_recv()
    apply_head(sib_seq)
    store(sib_seq)
    for e in range(half - 1):
        shard = (seq + n - 2 * (e + 1)) % n
        apply_head(shard)
        store(shard)
    for e in range(half - 1):
        late[e].wait_recv()
        shard = (sib_seq + n - 2 * (e + 1)) % n
        apply_head(shard)
        store(shard)

    for copy in stores:
        copy.wait()
    for copy in started:
        copy.wait_send()
    for d in range(1, n):
        feats[d].wait_send()

    @pl.when(seq >= half)
    def _():
        feats[0].wait_send()


def local(embeddings, skip_rows, w_query, w_key, w_value, w_out, conv_taps, w_head, head_bias):
    n = lax.axis_size("seq")
    n_win = lax.axis_size("win")
    n_grp = lax.axis_size("grp")
    _, tok, width = embeddings.shape
    cols = w_head.shape[1]
    piece = 2 * tok // n
    half = n // 2
    others = half - 1
    copies = PAIRS * (2 * others + 1) + 1 + 9 * others + 2
    bf16, f32 = jnp.bfloat16, jnp.float32
    dma = pltpu.SemaphoreType.DMA
    tracks = pl.pallas_call(
        functools.partial(kernel, n, n_win, n_grp),
        out_shape=jax.ShapeDtypeStruct((half, piece, n * cols), bf16),
        in_specs=[pl.BlockSpec(memory_space=pl.ANY)] * 9,
        out_specs=pl.BlockSpec(memory_space=pl.ANY),
        scratch_shapes=[
            pltpu.VMEM((tok, width), bf16),
            pltpu.VMEM((2 * tok, width), bf16),
            pltpu.VMEM(w_query.shape, bf16),
            pltpu.VMEM(w_key.shape, bf16),
            pltpu.VMEM(w_value.shape, bf16),
            pltpu.VMEM(w_out.shape, bf16),
            pltpu.VMEM(conv_taps.shape, f32),
            pltpu.VMEM((1, n * cols), f32),
            pltpu.VMEM((n, width, cols), bf16),
            pltpu.VMEM((tok, width), bf16),
            pltpu.VMEM((tok, HEADS * KEY), bf16),
            pltpu.VMEM((n, PAIRS, tok, KP + VP), bf16),
            pltpu.VMEM((tok, HEADS * VAL), bf16),
            pltpu.VMEM((width // 128, 2 * tok, 128), f32),
            pltpu.VMEM((tok, width), f32),
            pltpu.VMEM((tok, width), f32),
            pltpu.VMEM((2, 8, width), f32),
            pltpu.VMEM((2, 8, width), f32),
            pltpu.VMEM((n, piece, width), bf16),
            pltpu.VMEM((n, piece, width), bf16),
            pltpu.VMEM((tok, width), bf16),
            pltpu.VMEM((half, piece, n * cols), bf16),
            dma((9,)),
            dma((copies,)),
            dma((copies,)),
            dma((n,)),
            dma((n,)),
            dma((n,)),
        ],
        compiler_params=pltpu.CompilerParams(
            collective_id=0, has_side_effects=True, vmem_limit_bytes=60 * 1024 * 1024
        ),
    )(
        embeddings, skip_rows, w_query, w_key, w_value, w_out, conv_taps, w_head,
        head_bias.reshape(1, -1),
    )
    return tracks[None, :, None]


def solution(mesh):
    return jax.shard_map(
        local,
        mesh=mesh,
        in_specs=(
            P(("grp", "win"), "seq", None),
            P(("grp", "win"), "seq", None),
            P(),
            P(),
            P(),
            P(),
            P(),
            P(None, "seq"),
            P(),
        ),
        out_specs=P(("grp", "win"), None, "seq", None, None),
        check_vma=False,
    )
```

```python
import functools
import math

import jax
import jax.numpy as jnp
from jax import lax
from jax.experimental import pallas as pl
from jax.experimental.pallas import tpu as pltpu
from jax.sharding import PartitionSpec as P

HEADS = 4
KEY = 64
VAL = 192
PAIRS = HEADS // 2
KP = 2 * KEY
VP = 2 * VAL
TILE = 256
CHUNKS = 4
MESH = pl.DeviceIdType.MESH


def normalize(rows):
    centre = jnp.mean(rows, axis=-1, keepdims=True)
    centred = rows - centre
    spread = jnp.mean(centred * centred, axis=-1, keepdims=True)
    return centred * lax.rsqrt(spread + 1e-05)


def gelu(x):
    return 0.5 * x * (1.0 + lax.erf(x * math.sqrt(0.5)))


def kernel(
    n, n_win, n_grp,
    emb_h, skip_h, wq_h, wk_h, wv_h, wo_h, taps_h, wh_h, bias_h, out_h,
    x_v, skip_v, wq_v, wk_v, wv_v, wo_v, taps_v, bias_v, wh_v,
    normed_v, q_v, kv_v, att_v, wide_v, even_v, odd_v, halo_s, halo_r,
    feat_v, mid_v, got_v, blend_v, out_v,
    load_sem, send_sem, recv_sem, fsend_sem, frecv_sem, bsend_sem, brecv_sem, store_sem,
):
    grp = lax.axis_index("grp")
    win = lax.axis_index("win")
    seq = lax.axis_index("seq")
    tok, width = x_v.shape
    piece = feat_v.shape[1]
    cols = wh_v.shape[2]
    half = n // 2
    window_len = n * tok

    loads = {}
    for at, (name, src, dst) in enumerate(
        (
            ("x", emb_h.at[0], x_v),
            ("wk", wk_h, wk_v),
            ("wv", wv_h, wv_v),
            ("wq", wq_h, wq_v),
            ("skip", skip_h.at[0], skip_v),
            ("wo", wo_h, wo_v),
            ("taps", taps_h, taps_v),
            ("wh", wh_h, wh_v.at[seq]),
            ("bias", bias_h, bias_v),
        )
    ):
        loads[name] = pltpu.make_async_copy(src, dst, load_sem.at[at])
        loads[name].start()

    def dev(g, w, s):
        return (g, w, s)

    sibling = dev(grp, win, seq + 1 - 2 * (seq % 2))
    sib_seq = seq + 1 - 2 * (seq % 2)
    other_grp = 1 - grp
    other_win = win + 1 - 2 * (win % 2)
    across = dev(other_grp, win, seq)
    beside = dev(grp, other_win, seq)
    peers = [(seq + 2 * e) % n for e in range(1, half)]
    next_win = (win + 1) % n_win
    prev_win = (win + n_win - 1) % n_win

    barrier = pltpu.get_barrier_semaphore()
    greeted = [dev(grp, win, (seq + d) % n) for d in range(1, n)]
    greeted += [dev(grp, w, (seq + d) % n) for w in (next_win, prev_win) for d in range(n)]
    greeted.append(across)
    for target in greeted:
        pl.semaphore_signal(barrier, inc=1, device_id=target, device_id_type=MESH)
    pl.semaphore_wait(barrier, len(greeted))

    started = []

    def remote(src, dst, target):
        at = len(started)
        copy = pltpu.make_async_remote_copy(
            src_ref=src,
            dst_ref=dst,
            send_sem=send_sem.at[at],
            recv_sem=recv_sem.at[at],
            device_id=target,
            device_id_type=MESH,
        )
        copy.start()
        started.append(copy)
        return copy

    part = width // (2 * n_grp)
    chunk = part // CHUNKS

    def rows_of(g, w, c):
        return pl.ds(pl.multiple_of((g * 2 + w % 2) * part + c * chunk, chunk), chunk)

    def head_out(c):
        rows = rows_of(grp, win, c)
        return [remote(wh_h.at[rows], wh_v.at[seq, rows], dev(grp, win, p)) for p in peers]

    arrived = set()

    def arrive(copy):
        if id(copy) not in arrived:
            arrived.add(id(copy))
            copy.wait_recv()

    far_shards = [(seq + n - 2 * e) % n for e in range(1, half)]
    y_in, x_in, z_in, diag_in = {}, {}, {}, {}

    def head_spread(c):
        rows = rows_of(grp, win, c)
        x_in[c], z_in[c] = [], []
        for copy, shard in zip(y_in[c], far_shards):
            arrive(copy)
            block = wh_v.at[shard, rows]
            x_in[c].append(remote(block, block, across))
            z_in[c].append(remote(block, block, beside))

    def head_relay(c):
        diag_in[c] = []
        for e, shard in enumerate(far_shards):
            if c % 2 == 0:
                arrive(z_in[c][e])
                block = wh_v.at[shard, rows_of(grp, other_win, c)]
                diag_in[c].append(remote(block, block, across))
            else:
                arrive(x_in[c][e])
                block = wh_v.at[shard, rows_of(other_grp, win, c)]
                diag_in[c].append(remote(block, block, beside))

    late = [[] for _ in far_shards]

    def head_share(copies, g, w):
        for e, shard in enumerate(far_shards):
            for c in range(CHUNKS):
                arrive(copies[c][e])
            at = pl.ds(pl.multiple_of((g * 2 + w % 2) * part, part), part)
            block = wh_v.at[shard, at]
            late[e].append(remote(block, block, sibling))

    y_in[0] = head_out(0)

    loads["x"].wait()
    normed_v[...] = normalize(x_v[...].astype(jnp.float32)).astype(jnp.bfloat16)
    loads["wk"].wait()
    loads["wv"].wait()
    kv_far, kv_near = [], []
    for p in range(PAIRS):
        kv_v[seq, p, :, :KP] = jnp.dot(
            normed_v[...], wk_v[:, p * KP : (p + 1) * KP], preferred_element_type=jnp.float32
        ).astype(jnp.bfloat16)
        kv_v[seq, p, :, KP:] = jnp.dot(
            normed_v[...], wv_v[:, p * VP : (p + 1) * VP], preferred_element_type=jnp.float32
        ).astype(jnp.bfloat16)
        block = kv_v.at[seq, p]
        kv_far.append([remote(block, block, dev(grp, win, s)) for s in peers])
        kv_near.append([remote(block, block, sibling)])
    for c in range(1, CHUNKS):
        y_in[c] = head_out(c)
    loads["wq"].wait()
    q_v[...] = jnp.dot(normed_v[...], wq_v[...], preferred_element_type=jnp.float32).astype(
        jnp.bfloat16
    )
    loads["skip"].wait()
    for j in range(width // 128):
        wide_v[j] = skip_v[:, j * 128 : (j + 1) * 128].astype(jnp.float32)

    def kv_relay(p):
        for e in range(half - 1):
            kv_far[p][e].wait_recv()
            block = kv_v.at[(seq + n - 2 * (e + 1)) % n, p]
            kv_near[p].append(remote(block, block, sibling))

    def attend(p):
        for copy in kv_near[p]:
            copy.wait_recv()
        keys = kv_v[:, p, :, :KP].reshape(n * tok, KP)
        vals = kv_v[:, p, :, KP:].reshape(n * tok, VP)
        pair = q_v[:, p * KP : (p + 1) * KP]
        key_lane = lax.broadcasted_iota(jnp.int32, (tok, KP), 1)
        outs = []
        for h in range(2):
            mine = key_lane < KEY if h == 0 else key_lane >= KEY
            masked = jnp.where(mine, pair.astype(jnp.float32), 0.0).astype(jnp.bfloat16)
            scores = lax.dot_general(
                masked, keys, (((1,), (1,)), ((), ())), preferred_element_type=jnp.float32
            ) * (1.0 / math.sqrt(KEY))
            expo = jnp.exp(scores - jnp.max(scores, axis=-1, keepdims=True))
            denom = jnp.sum(expo, axis=-1, keepdims=True)
            outs.append(
                jnp.dot(expo.astype(jnp.bfloat16), vals, preferred_element_type=jnp.float32) / denom
            )
        val_lane = lax.broadcasted_iota(jnp.int32, (tok, VP), 1)
        att_v[:, p * VP : (p + 1) * VP] = jnp.where(val_lane < VAL, outs[0], outs[1]).astype(
            jnp.bfloat16
        )

    kv_relay(0)
    head_spread(0)
    attend(0)
    for p in range(1, PAIRS):
        kv_relay(p)
        attend(p)
    head_spread(1)
    head_relay(0)
    own_sib = remote(wh_h, wh_v.at[seq], sibling)
    loads["wo"].wait()

    def up_step(t, carry):
        at = pl.ds(pl.multiple_of(t * TILE, TILE), TILE)
        resid = x_v[:, at].astype(jnp.float32) + jnp.dot(
            att_v[...], wo_v[:, at], preferred_element_type=jnp.float32
        )
        for m in range(2):
            here = pl.ds(pl.multiple_of(t * TILE + m * 128, 128), 128)
            mine = resid[:, m * 128 : (m + 1) * 128]
            even = (mine + wide_v[t * (TILE // 128) + m, pl.ds(0, tok, stride=2), :]).astype(jnp.bfloat16)
            odd = (mine + wide_v[t * (TILE // 128) + m, pl.ds(1, tok, stride=2), :]).astype(jnp.bfloat16)
            even = even.astype(jnp.float32)
            odd = odd.astype(jnp.float32)
            even_v[:, here] = even
            odd_v[:, here] = odd
            halo_s[0, :, here] = even[:8]
            halo_s[1, :, here] = odd[tok - 8 :]
        return carry

    lax.fori_loop(0, width // TILE, up_step, 0)
    to_prev = remote(halo_s.at[0], halo_r.at[0], dev(grp, win, (seq + n - 1) % n))
    to_next = remote(halo_s.at[1], halo_r.at[1], dev(grp, win, (seq + 1) % n))
    head_spread(2)
    loads["taps"].wait()
    to_prev.wait_recv()
    to_next.wait_recv()

    def conv_step(t, carry):
        at = pl.ds(pl.multiple_of(t * 128, 128), 128)
        even = even_v[:, at]
        odd = odd_v[:, at]
        row = lax.broadcasted_iota(jnp.int32, (tok, 128), 0)
        before = jnp.where(seq == 0, 0.0, halo_r[1, 7:8, at])
        after = jnp.where(seq == n - 1, 0.0, halo_r[0, 0:1, at])
        odd_prev = jnp.where(row == 0, before, pltpu.roll(odd, 1, axis=0))
        even_next = jnp.where(row == tok - 1, after, pltpu.roll(even, tok - 1, axis=0))
        t0, t1, t2 = taps_v[0:1, at], taps_v[1:2, at], taps_v[2:3, at]
        first = t0 * odd_prev + t1 * even + t2 * odd
        second = t0 * even + t1 * odd + t2 * even_next
        wide_v[t, pl.ds(0, tok, stride=2), :] = gelu(first)
        wide_v[t, pl.ds(1, tok, stride=2), :] = gelu(second)
        return carry

    lax.fori_loop(0, width // 128, conv_step, 0)
    for k in range(n):
        for j in range(width // 128):
            feat_v[k, :, j * 128 : (j + 1) * 128] = wide_v[
                j, k * piece : (k + 1) * piece, :
            ].astype(jnp.bfloat16)

    feats = []
    for d in list(range(half, n)) + list(range(1, half)):
        owner = (seq + d) % n
        feats.append(
            pltpu.make_async_remote_copy(
                src_ref=feat_v.at[owner],
                dst_ref=mid_v.at[seq],
                send_sem=fsend_sem.at[d],
                recv_sem=frecv_sem.at[seq],
                device_id=dev(grp, win, owner),
                device_id_type=MESH,
            )
        )
        feats[-1].start()
    mid_v[seq] = feat_v[seq]

    def feature_wait(slot):
        pltpu.make_async_remote_copy(
            src_ref=feat_v.at[slot],
            dst_ref=mid_v.at[slot],
            send_sem=fsend_sem.at[0],
            recv_sem=frecv_sem.at[slot],
            device_id=dev(grp, win, slot),
            device_id_type=MESH,
        ).wait_recv()

    behind = []

    def feature_forward(i):
        at = (seq + i) % half
        if i == 0:

            @pl.when(seq < half)
            def _():
                feature_wait(half + at)

        else:
            feature_wait(half + at)
        behind.append(
            pltpu.make_async_remote_copy(
                src_ref=mid_v.at[half + at],
                dst_ref=got_v.at[at],
                send_sem=bsend_sem.at[i],
                recv_sem=brecv_sem.at[i],
                device_id=dev(grp, next_win, seq),
                device_id_type=MESH,
            )
        )
        behind[-1].start()

    head_spread(3)
    head_share(y_in, grp, win)
    head_relay(1)
    head_relay(2)
    feature_forward(0)
    head_relay(3)
    for i in range(1, half):
        feature_forward(i)
    loads["wh"].wait()
    head_share(x_in, other_grp, win)
    head_share(z_in, grp, other_win)
    head_share(diag_in, other_grp, other_win)
    loads["bias"].wait()

    for i in range(half):
        at = (seq + i) % half
        if i == 0:

            @pl.when(seq >= half)
            def _():
                feature_wait(at)

        else:
            feature_wait(at)
    for copy in behind:
        copy.wait_recv()

    def blend_step(t, carry):
        at = pl.ds(pl.multiple_of(t * 128, 128), 128)
        blocks = []
        for i in range(half):
            place = lax.broadcasted_iota(jnp.int32, (piece, 128), 0) + (i * n + seq) * piece
            place = place.astype(jnp.float32)
            blocks.append(
                (
                    (place + 1.0) * mid_v[i, :, at].astype(jnp.float32)
                    + (window_len - place) * got_v[i, :, at].astype(jnp.float32)
                )
                * (1.0 / (window_len + 1.0))
            )
        blend_v[:, at] = jnp.concatenate(blocks, axis=0).astype(jnp.bfloat16)
        return carry

    lax.fori_loop(0, width // 128, blend_step, 0)

    def apply_head(shard):
        def head_step(t, carry):
            at = pl.ds(pl.multiple_of(t * TILE, TILE), TILE)
            base = pl.ds(pl.multiple_of(shard * cols + t * TILE, TILE), TILE)
            z = (
                jnp.dot(blend_v[...], wh_v[shard, :, at], preferred_element_type=jnp.float32)
                + bias_v[:, base]
            )
            z = jnp.maximum(z, 0.0) + jnp.log1p(jnp.exp(-jnp.abs(z)))
            for i in range(half):
                out_v[i, :, base] = z[i * piece : (i + 1) * piece].astype(jnp.bfloat16)
            return carry

        lax.fori_loop(0, cols // TILE, head_step, 0)

    stores = []

    def store(shard):
        base = pl.ds(pl.multiple_of(shard * cols, cols), cols)
        at = len(stores)
        stores.append(
            pltpu.make_async_copy(out_v.at[:, :, base], out_h.at[:, :, base], store_sem.at[at])
        )
        stores[at].start()

    apply_head(seq)
    store(seq)
    own_sib.wait_recv()
    apply_head(sib_seq)
    store(sib_seq)
    for e in range(half - 1):
        shard = (seq + n - 2 * (e + 1)) % n
        apply_head(shard)
        store(shard)
    for e in range(half - 1):
        for copy in late[e]:
            copy.wait_recv()
        shard = (sib_seq + n - 2 * (e + 1)) % n
        apply_head(shard)
        store(shard)

    for copy in stores:
        copy.wait()
    for copy in started:
        copy.wait_send()
    for copy in feats + behind:
        copy.wait_send()


def local(embeddings, skip_rows, w_query, w_key, w_value, w_out, conv_taps, w_head, head_bias):
    n = lax.axis_size("seq")
    n_win = lax.axis_size("win")
    n_grp = lax.axis_size("grp")
    _, tok, width = embeddings.shape
    cols = w_head.shape[1]
    piece = 2 * tok // n
    half = n // 2
    others = half - 1
    copies = PAIRS * (2 * others + 1) + 1 + (4 * CHUNKS + 4) * others + 2
    bf16, f32 = jnp.bfloat16, jnp.float32
    dma = pltpu.SemaphoreType.DMA
    tracks = pl.pallas_call(
        functools.partial(kernel, n, n_win, n_grp),
        out_shape=jax.ShapeDtypeStruct((half, piece, n * cols), bf16),
        in_specs=[pl.BlockSpec(memory_space=pl.ANY)] * 9,
        out_specs=pl.BlockSpec(memory_space=pl.ANY),
        scratch_shapes=[
            pltpu.VMEM((tok, width), bf16),
            pltpu.VMEM((2 * tok, width), bf16),
            pltpu.VMEM(w_query.shape, bf16),
            pltpu.VMEM(w_key.shape, bf16),
            pltpu.VMEM(w_value.shape, bf16),
            pltpu.VMEM(w_out.shape, bf16),
            pltpu.VMEM(conv_taps.shape, f32),
            pltpu.VMEM((1, n * cols), f32),
            pltpu.VMEM((n, width, cols), bf16),
            pltpu.VMEM((tok, width), bf16),
            pltpu.VMEM((tok, HEADS * KEY), bf16),
            pltpu.VMEM((n, PAIRS, tok, KP + VP), bf16),
            pltpu.VMEM((tok, HEADS * VAL), bf16),
            pltpu.VMEM((width // 128, 2 * tok, 128), f32),
            pltpu.VMEM((tok, width), f32),
            pltpu.VMEM((tok, width), f32),
            pltpu.VMEM((2, 8, width), f32),
            pltpu.VMEM((2, 8, width), f32),
            pltpu.VMEM((n, piece, width), bf16),
            pltpu.VMEM((n, piece, width), bf16),
            pltpu.VMEM((half, piece, width), bf16),
            pltpu.VMEM((tok, width), bf16),
            pltpu.VMEM((half, piece, n * cols), bf16),
            dma((9,)),
            dma((copies,)),
            dma((copies,)),
            dma((n,)),
            dma((n,)),
            dma((half,)),
            dma((half,)),
            dma((n,)),
        ],
        compiler_params=pltpu.CompilerParams(
            collective_id=0, has_side_effects=True, vmem_limit_bytes=60 * 1024 * 1024
        ),
    )(
        embeddings, skip_rows, w_query, w_key, w_value, w_out, conv_taps, w_head,
        head_bias.reshape(1, -1),
    )
    return tracks[None, :, None]


def solution(mesh):
    return jax.shard_map(
        local,
        mesh=mesh,
        in_specs=(
            P(("grp", "win"), "seq", None),
            P(("grp", "win"), "seq", None),
            P(),
            P(),
            P(),
            P(),
            P(),
            P(None, "seq"),
            P(),
        ),
        out_specs=P(("grp", "win"), None, "seq", None, None),
        check_vma=False,
    )
```

```python
import functools
import math

import jax
import jax.numpy as jnp
from jax import lax
from jax.experimental import pallas as pl
from jax.experimental.pallas import tpu as pltpu
from jax.sharding import PartitionSpec as P

HEADS = 4
KEY = 64
VAL = 192
PAIRS = HEADS // 2
KP = 2 * KEY
VP = 2 * VAL
TILE = 256
CHUNKS = 4
BANDS = 4
MESH = pl.DeviceIdType.MESH


def normalize(rows):
    centre = jnp.mean(rows, axis=-1, keepdims=True)
    centred = rows - centre
    spread = jnp.mean(centred * centred, axis=-1, keepdims=True)
    return centred * lax.rsqrt(spread + 1e-05)


def gelu(x):
    return 0.5 * x * (1.0 + lax.erf(x * math.sqrt(0.5)))


def kernel(
    n, n_win, n_grp,
    emb_h, skip_h, wq_h, wk_h, wv_h, wo_h, taps_h, wh_h, bias_h, out_h,
    x_v, skip_v, wq_v, wk_v, wv_v, wo_v, taps_v, bias_v, wh_v,
    normed_v, q_v, kv_v, att_v, wide_v, even_v, odd_v, halo_s, halo_r,
    feat_v, mid_v, got_v, blend_v, out_v,
    load_sem, send_sem, recv_sem, fsend_sem, frecv_sem, bsend_sem, brecv_sem, store_sem,
):
    grp = lax.axis_index("grp")
    win = lax.axis_index("win")
    seq = lax.axis_index("seq")
    tok, width = x_v.shape
    piece = feat_v.shape[1]
    cols = wh_v.shape[2]
    half = n // 2
    window_len = n * tok

    loads = {}
    for at, (name, src, dst) in enumerate(
        (
            ("x", emb_h.at[0], x_v),
            ("wk", wk_h, wk_v),
            ("wv", wv_h, wv_v),
            ("wq", wq_h, wq_v),
            ("skip", skip_h.at[0], skip_v),
            ("wo", wo_h, wo_v),
            ("taps", taps_h, taps_v),
            ("wh", wh_h, wh_v.at[seq]),
            ("bias", bias_h, bias_v),
        )
    ):
        loads[name] = pltpu.make_async_copy(src, dst, load_sem.at[at])
        loads[name].start()

    def dev(g, w, s):
        return (g, w, s)

    sibling = dev(grp, win, seq + 1 - 2 * (seq % 2))
    sib_seq = seq + 1 - 2 * (seq % 2)
    other_grp = 1 - grp
    other_win = win + 1 - 2 * (win % 2)
    across = dev(other_grp, win, seq)
    beside = dev(grp, other_win, seq)
    peers = [(seq + 2 * e) % n for e in range(1, half)]
    next_win = (win + 1) % n_win
    prev_win = (win + n_win - 1) % n_win

    barrier = pltpu.get_barrier_semaphore()
    greeted = [dev(grp, win, (seq + d) % n) for d in range(1, n)]
    greeted += [dev(grp, w, (seq + d) % n) for w in (next_win, prev_win) for d in range(n)]
    greeted.append(across)
    for target in greeted:
        pl.semaphore_signal(barrier, inc=1, device_id=target, device_id_type=MESH)
    pl.semaphore_wait(barrier, len(greeted))

    started = []

    def remote(src, dst, target):
        at = len(started)
        copy = pltpu.make_async_remote_copy(
            src_ref=src,
            dst_ref=dst,
            send_sem=send_sem.at[at],
            recv_sem=recv_sem.at[at],
            device_id=target,
            device_id_type=MESH,
        )
        copy.start()
        started.append(copy)
        return copy

    part = width // (2 * n_grp)
    chunk = part // CHUNKS

    def rows_of(g, w, c):
        return pl.ds(pl.multiple_of((g * 2 + w % 2) * part + c * chunk, chunk), chunk)

    def head_out(c):
        rows = rows_of(grp, win, c)
        return [remote(wh_h.at[rows], wh_v.at[seq, rows], dev(grp, win, p)) for p in peers]

    arrived = set()

    def arrive(copy):
        if id(copy) not in arrived:
            arrived.add(id(copy))
            copy.wait_recv()

    far_shards = [(seq + n - 2 * e) % n for e in range(1, half)]
    y_in, x_in, z_in, diag_in = {}, {}, {}, {}

    def head_spread(c):
        rows = rows_of(grp, win, c)
        x_in[c], z_in[c] = [], []
        for copy, shard in zip(y_in[c], far_shards):
            arrive(copy)
            block = wh_v.at[shard, rows]
            x_in[c].append(remote(block, block, across))
            z_in[c].append(remote(block, block, beside))

    def head_relay(c):
        diag_in[c] = []
        for e, shard in enumerate(far_shards):
            if c % 2 == 0:
                arrive(z_in[c][e])
                block = wh_v.at[shard, rows_of(grp, other_win, c)]
                diag_in[c].append(remote(block, block, across))
            else:
                arrive(x_in[c][e])
                block = wh_v.at[shard, rows_of(other_grp, win, c)]
                diag_in[c].append(remote(block, block, beside))

    late = [[] for _ in far_shards]

    def head_share(copies, g, w):
        for e, shard in enumerate(far_shards):
            for c in range(CHUNKS):
                arrive(copies[c][e])
            at = pl.ds(pl.multiple_of((g * 2 + w % 2) * part, part), part)
            block = wh_v.at[shard, at]
            late[e].append(remote(block, block, sibling))

    y_in[0] = head_out(0)

    loads["x"].wait()
    normed_v[...] = normalize(x_v[...].astype(jnp.float32)).astype(jnp.bfloat16)
    loads["wk"].wait()
    loads["wv"].wait()
    kv_far, kv_near = [], []
    for p in range(PAIRS):
        kv_v[seq, p, :, :KP] = jnp.dot(
            normed_v[...], wk_v[:, p * KP : (p + 1) * KP], preferred_element_type=jnp.float32
        ).astype(jnp.bfloat16)
        kv_v[seq, p, :, KP:] = jnp.dot(
            normed_v[...], wv_v[:, p * VP : (p + 1) * VP], preferred_element_type=jnp.float32
        ).astype(jnp.bfloat16)
        block = kv_v.at[seq, p]
        kv_far.append([remote(block, block, dev(grp, win, s)) for s in peers])
        kv_near.append([remote(block, block, sibling)])
    y_in[1] = head_out(1)
    loads["wq"].wait()
    q_v[...] = jnp.dot(normed_v[...], wq_v[...], preferred_element_type=jnp.float32).astype(
        jnp.bfloat16
    )
    loads["skip"].wait()
    for j in range(width // 128):
        wide_v[j] = skip_v[:, j * 128 : (j + 1) * 128].astype(jnp.float32)

    def kv_relay(p):
        for e in range(half - 1):
            kv_far[p][e].wait_recv()
            block = kv_v.at[(seq + n - 2 * (e + 1)) % n, p]
            kv_near[p].append(remote(block, block, sibling))

    def attend(p):
        for copy in kv_near[p]:
            copy.wait_recv()
        keys = kv_v[:, p, :, :KP].reshape(n * tok, KP)
        vals = kv_v[:, p, :, KP:].reshape(n * tok, VP)
        pair = q_v[:, p * KP : (p + 1) * KP]
        key_lane = lax.broadcasted_iota(jnp.int32, (tok, KP), 1)
        outs = []
        for h in range(2):
            mine = key_lane < KEY if h == 0 else key_lane >= KEY
            masked = jnp.where(mine, pair.astype(jnp.float32), 0.0).astype(jnp.bfloat16)
            scores = lax.dot_general(
                masked, keys, (((1,), (1,)), ((), ())), preferred_element_type=jnp.float32
            ) * (1.0 / math.sqrt(KEY))
            expo = jnp.exp(scores - jnp.max(scores, axis=-1, keepdims=True))
            denom = jnp.sum(expo, axis=-1, keepdims=True)
            outs.append(
                jnp.dot(expo.astype(jnp.bfloat16), vals, preferred_element_type=jnp.float32) / denom
            )
        val_lane = lax.broadcasted_iota(jnp.int32, (tok, VP), 1)
        att_v[:, p * VP : (p + 1) * VP] = jnp.where(val_lane < VAL, outs[0], outs[1]).astype(
            jnp.bfloat16
        )

    kv_relay(0)
    head_spread(0)
    attend(0)
    for p in range(1, PAIRS):
        kv_relay(p)
        attend(p)
    head_spread(1)
    head_relay(0)
    own_sib = remote(wh_h, wh_v.at[seq], sibling)
    loads["wo"].wait()

    def up_step(t, carry):
        at = pl.ds(pl.multiple_of(t * TILE, TILE), TILE)
        resid = x_v[:, at].astype(jnp.float32) + jnp.dot(
            att_v[...], wo_v[:, at], preferred_element_type=jnp.float32
        )
        for m in range(2):
            here = pl.ds(pl.multiple_of(t * TILE + m * 128, 128), 128)
            mine = resid[:, m * 128 : (m + 1) * 128]
            even = (mine + wide_v[t * (TILE // 128) + m, pl.ds(0, tok, stride=2), :]).astype(jnp.bfloat16)
            odd = (mine + wide_v[t * (TILE // 128) + m, pl.ds(1, tok, stride=2), :]).astype(jnp.bfloat16)
            even = even.astype(jnp.float32)
            odd = odd.astype(jnp.float32)
            even_v[:, here] = even
            odd_v[:, here] = odd
            halo_s[0, :, here] = even[:8]
            halo_s[1, :, here] = odd[tok - 8 :]
        return carry

    lax.fori_loop(0, width // TILE, up_step, 0)
    to_prev = remote(halo_s.at[0], halo_r.at[0], dev(grp, win, (seq + n - 1) % n))
    to_next = remote(halo_s.at[1], halo_r.at[1], dev(grp, win, (seq + 1) % n))
    for c in range(2, CHUNKS):
        y_in[c] = head_out(c)
    loads["taps"].wait()
    to_prev.wait_recv()
    to_next.wait_recv()

    def conv_step(t, carry):
        at = pl.ds(pl.multiple_of(t * 128, 128), 128)
        even = even_v[:, at]
        odd = odd_v[:, at]
        row = lax.broadcasted_iota(jnp.int32, (tok, 128), 0)
        before = jnp.where(seq == 0, 0.0, halo_r[1, 7:8, at])
        after = jnp.where(seq == n - 1, 0.0, halo_r[0, 0:1, at])
        odd_prev = jnp.where(row == 0, before, pltpu.roll(odd, 1, axis=0))
        even_next = jnp.where(row == tok - 1, after, pltpu.roll(even, tok - 1, axis=0))
        t0, t1, t2 = taps_v[0:1, at], taps_v[1:2, at], taps_v[2:3, at]
        first = t0 * odd_prev + t1 * even + t2 * odd
        second = t0 * even + t1 * odd + t2 * even_next
        wide_v[t, pl.ds(0, tok, stride=2), :] = gelu(first)
        wide_v[t, pl.ds(1, tok, stride=2), :] = gelu(second)
        return carry

    band = width // BANDS
    lanes = band // 128
    feats = []
    for b in range(BANDS):
        lax.fori_loop(b * lanes, (b + 1) * lanes, conv_step, 0)
        for k in range(n):
            for j in range(b * lanes, (b + 1) * lanes):
                feat_v[k, :, j * 128 : (j + 1) * 128] = wide_v[
                    j, k * piece : (k + 1) * piece, :
                ].astype(jnp.bfloat16)
        span = pl.ds(b * band, band)
        for d in list(range(half, n)) + list(range(1, half)):
            owner = (seq + d) % n
            feats.append(
                pltpu.make_async_remote_copy(
                    src_ref=feat_v.at[owner, :, span],
                    dst_ref=mid_v.at[seq, :, span],
                    send_sem=fsend_sem.at[d, b],
                    recv_sem=frecv_sem.at[seq, b],
                    device_id=dev(grp, win, owner),
                    device_id_type=MESH,
                )
            )
            feats[-1].start()
        mid_v[seq, :, span] = feat_v[seq, :, span]
        if b == 1:
            head_spread(2)

    def feature_wait(slot, b):
        span = pl.ds(b * band, band)
        pltpu.make_async_remote_copy(
            src_ref=feat_v.at[slot, :, span],
            dst_ref=mid_v.at[slot, :, span],
            send_sem=fsend_sem.at[0, b],
            recv_sem=frecv_sem.at[slot, b],
            device_id=dev(grp, win, slot),
            device_id_type=MESH,
        ).wait_recv()

    behind = []

    def feature_forward(b):
        span = pl.ds(b * band, band)
        for i in range(half):
            at = (seq + i) % half
            if i == 0:

                @pl.when(seq < half)
                def _():
                    feature_wait(half + at, b)

            else:
                feature_wait(half + at, b)
            behind.append(
                pltpu.make_async_remote_copy(
                    src_ref=mid_v.at[half + at, :, span],
                    dst_ref=got_v.at[at, :, span],
                    send_sem=bsend_sem.at[i, b],
                    recv_sem=brecv_sem.at[i, b],
                    device_id=dev(grp, next_win, seq),
                    device_id_type=MESH,
                )
            )
            behind[-1].start()

    head_relay(1)
    head_spread(3)
    feature_forward(0)
    head_relay(2)
    feature_forward(1)
    head_relay(3)
    for b in range(2, BANDS):
        feature_forward(b)
    head_share(y_in, grp, win)
    loads["wh"].wait()
    head_share(x_in, other_grp, win)
    head_share(z_in, grp, other_win)
    head_share(diag_in, other_grp, other_win)
    loads["bias"].wait()

    for i in range(half):
        at = (seq + i) % half
        for b in range(BANDS):
            if i == 0:

                @pl.when(seq >= half)
                def _():
                    feature_wait(at, b)

            else:
                feature_wait(at, b)
    for copy in behind:
        copy.wait_recv()

    def blend_step(t, carry):
        at = pl.ds(pl.multiple_of(t * 128, 128), 128)
        blocks = []
        for i in range(half):
            place = lax.broadcasted_iota(jnp.int32, (piece, 128), 0) + (i * n + seq) * piece
            place = place.astype(jnp.float32)
            blocks.append(
                (
                    (place + 1.0) * mid_v[i, :, at].astype(jnp.float32)
                    + (window_len - place) * got_v[i, :, at].astype(jnp.float32)
                )
                * (1.0 / (window_len + 1.0))
            )
        blend_v[:, at] = jnp.concatenate(blocks, axis=0).astype(jnp.bfloat16)
        return carry

    lax.fori_loop(0, width // 128, blend_step, 0)

    def apply_head(shard):
        def head_step(t, carry):
            at = pl.ds(pl.multiple_of(t * TILE, TILE), TILE)
            base = pl.ds(pl.multiple_of(shard * cols + t * TILE, TILE), TILE)
            z = (
                jnp.dot(blend_v[...], wh_v[shard, :, at], preferred_element_type=jnp.float32)
                + bias_v[:, base]
            )
            z = jnp.maximum(z, 0.0) + jnp.log1p(jnp.exp(-jnp.abs(z)))
            for i in range(half):
                out_v[i, :, base] = z[i * piece : (i + 1) * piece].astype(jnp.bfloat16)
            return carry

        lax.fori_loop(0, cols // TILE, head_step, 0)

    stores = []

    def store(shard):
        base = pl.ds(pl.multiple_of(shard * cols, cols), cols)
        at = len(stores)
        stores.append(
            pltpu.make_async_copy(out_v.at[:, :, base], out_h.at[:, :, base], store_sem.at[at])
        )
        stores[at].start()

    apply_head(seq)
    store(seq)
    own_sib.wait_recv()
    apply_head(sib_seq)
    store(sib_seq)
    for e in range(half - 1):
        shard = (seq + n - 2 * (e + 1)) % n
        apply_head(shard)
        store(shard)
    for e in range(half - 1):
        for copy in late[e]:
            copy.wait_recv()
        shard = (sib_seq + n - 2 * (e + 1)) % n
        apply_head(shard)
        store(shard)

    for copy in stores:
        copy.wait()
    for copy in started:
        copy.wait_send()
    for copy in feats + behind:
        copy.wait_send()


def local(embeddings, skip_rows, w_query, w_key, w_value, w_out, conv_taps, w_head, head_bias):
    n = lax.axis_size("seq")
    n_win = lax.axis_size("win")
    n_grp = lax.axis_size("grp")
    _, tok, width = embeddings.shape
    cols = w_head.shape[1]
    piece = 2 * tok // n
    half = n // 2
    others = half - 1
    copies = PAIRS * (2 * others + 1) + 1 + (4 * CHUNKS + 4) * others + 2
    bf16, f32 = jnp.bfloat16, jnp.float32
    dma = pltpu.SemaphoreType.DMA
    tracks = pl.pallas_call(
        functools.partial(kernel, n, n_win, n_grp),
        out_shape=jax.ShapeDtypeStruct((half, piece, n * cols), bf16),
        in_specs=[pl.BlockSpec(memory_space=pl.ANY)] * 9,
        out_specs=pl.BlockSpec(memory_space=pl.ANY),
        scratch_shapes=[
            pltpu.VMEM((tok, width), bf16),
            pltpu.VMEM((2 * tok, width), bf16),
            pltpu.VMEM(w_query.shape, bf16),
            pltpu.VMEM(w_key.shape, bf16),
            pltpu.VMEM(w_value.shape, bf16),
            pltpu.VMEM(w_out.shape, bf16),
            pltpu.VMEM(conv_taps.shape, f32),
            pltpu.VMEM((1, n * cols), f32),
            pltpu.VMEM((n, width, cols), bf16),
            pltpu.VMEM((tok, width), bf16),
            pltpu.VMEM((tok, HEADS * KEY), bf16),
            pltpu.VMEM((n, PAIRS, tok, KP + VP), bf16),
            pltpu.VMEM((tok, HEADS * VAL), bf16),
            pltpu.VMEM((width // 128, 2 * tok, 128), f32),
            pltpu.VMEM((tok, width), f32),
            pltpu.VMEM((tok, width), f32),
            pltpu.VMEM((2, 8, width), f32),
            pltpu.VMEM((2, 8, width), f32),
            pltpu.VMEM((n, piece, width), bf16),
            pltpu.VMEM((n, piece, width), bf16),
            pltpu.VMEM((half, piece, width), bf16),
            pltpu.VMEM((tok, width), bf16),
            pltpu.VMEM((half, piece, n * cols), bf16),
            dma((9,)),
            dma((copies,)),
            dma((copies,)),
            dma((n, BANDS)),
            dma((n, BANDS)),
            dma((half, BANDS)),
            dma((half, BANDS)),
            dma((n,)),
        ],
        compiler_params=pltpu.CompilerParams(
            collective_id=0, has_side_effects=True, vmem_limit_bytes=60 * 1024 * 1024
        ),
    )(
        embeddings, skip_rows, w_query, w_key, w_value, w_out, conv_taps, w_head,
        head_bias.reshape(1, -1),
    )
    return tracks[None, :, None]


def solution(mesh):
    return jax.shard_map(
        local,
        mesh=mesh,
        in_specs=(
            P(("grp", "win"), "seq", None),
            P(("grp", "win"), "seq", None),
            P(),
            P(),
            P(),
            P(),
            P(),
            P(None, "seq"),
            P(),
        ),
        out_specs=P(("grp", "win"), None, "seq", None, None),
        check_vma=False,
    )
```

```python
import functools
import math

import jax
import jax.numpy as jnp
from jax import lax
from jax.experimental import pallas as pl
from jax.experimental.pallas import tpu as pltpu
from jax.sharding import PartitionSpec as P

HEADS = 4
KEY = 64
VAL = 192
PAIRS = HEADS // 2
KP = 2 * KEY
VP = 2 * VAL
TILE = 256
CHUNKS = 4
BANDS = 4
MESH = pl.DeviceIdType.MESH


def normalize(rows):
    centre = jnp.mean(rows, axis=-1, keepdims=True)
    centred = rows - centre
    spread = jnp.mean(centred * centred, axis=-1, keepdims=True)
    return centred * lax.rsqrt(spread + 1e-05)


def gelu(x):
    return 0.5 * x * (1.0 + lax.erf(x * math.sqrt(0.5)))


def kernel(
    n, n_win, n_grp,
    emb_h, skip_h, wq_h, wk_h, wv_h, wo_h, taps_h, wh_h, bias_h, out_h,
    x_v, skip_v, wq_v, wk_v, wv_v, wo_v, taps_v, bias_v, wh_v,
    normed_v, q_v, kv_v, att_v, wide_v, even_v, odd_v, halo_s, halo_r,
    feat_v, mid_v, got_v, blend_v, out_v,
    load_sem, send_sem, recv_sem, fsend_sem, frecv_sem, bsend_sem, brecv_sem, store_sem,
):
    grp = lax.axis_index("grp")
    win = lax.axis_index("win")
    seq = lax.axis_index("seq")
    tok, width = x_v.shape
    piece = feat_v.shape[1]
    cols = wh_v.shape[2]
    half = n // 2
    window_len = n * tok

    loads = {}
    for at, (name, src, dst) in enumerate(
        (
            ("x", emb_h.at[0], x_v),
            ("wk", wk_h, wk_v),
            ("wv", wv_h, wv_v),
            ("wq", wq_h, wq_v),
            ("skip", skip_h.at[0], skip_v),
            ("wo", wo_h, wo_v),
            ("taps", taps_h, taps_v),
            ("wh", wh_h, wh_v.at[seq]),
            ("bias", bias_h, bias_v),
        )
    ):
        loads[name] = pltpu.make_async_copy(src, dst, load_sem.at[at])
        loads[name].start()

    def dev(g, w, s):
        return (g, w, s)

    sibling = dev(grp, win, seq + 1 - 2 * (seq % 2))
    sib_seq = seq + 1 - 2 * (seq % 2)
    other_grp = 1 - grp
    other_win = win + 1 - 2 * (win % 2)
    across = dev(other_grp, win, seq)
    beside = dev(grp, other_win, seq)
    peers = [(seq + 2 * e) % n for e in range(1, half)]
    next_win = (win + 1) % n_win
    prev_win = (win + n_win - 1) % n_win

    barrier = pltpu.get_barrier_semaphore()
    greeted = [dev(grp, win, (seq + d) % n) for d in range(1, n)]
    greeted += [dev(grp, w, (seq + d) % n) for w in (next_win, prev_win) for d in range(n)]
    greeted.append(across)
    for target in greeted:
        pl.semaphore_signal(barrier, inc=1, device_id=target, device_id_type=MESH)
    pl.semaphore_wait(barrier, len(greeted))

    started = []

    def remote(src, dst, target):
        at = len(started)
        copy = pltpu.make_async_remote_copy(
            src_ref=src,
            dst_ref=dst,
            send_sem=send_sem.at[at],
            recv_sem=recv_sem.at[at],
            device_id=target,
            device_id_type=MESH,
        )
        copy.start()
        started.append(copy)
        return copy

    part = width // (2 * n_grp)
    chunk = part // CHUNKS

    def rows_of(g, w, c):
        return pl.ds(pl.multiple_of((g * 2 + w % 2) * part + c * chunk, chunk), chunk)

    def head_out(c):
        rows = rows_of(grp, win, c)
        return [remote(wh_h.at[rows], wh_v.at[seq, rows], dev(grp, win, p)) for p in peers]

    arrived = set()

    def arrive(copy):
        if id(copy) not in arrived:
            arrived.add(id(copy))
            copy.wait_recv()

    far_shards = [(seq + n - 2 * e) % n for e in range(1, half)]
    y_in, x_in, z_in, diag_in = {}, {}, {}, {}

    def head_spread(c):
        rows = rows_of(grp, win, c)
        x_in[c], z_in[c] = [], []
        for copy, shard in zip(y_in[c], far_shards):
            arrive(copy)
            block = wh_v.at[shard, rows]
            x_in[c].append(remote(block, block, across))
            z_in[c].append(remote(block, block, beside))

    def head_relay(c):
        diag_in[c] = []
        for e, shard in enumerate(far_shards):
            if c % 2 == 0:
                arrive(z_in[c][e])
                block = wh_v.at[shard, rows_of(grp, other_win, c)]
                diag_in[c].append(remote(block, block, across))
            else:
                arrive(x_in[c][e])
                block = wh_v.at[shard, rows_of(other_grp, win, c)]
                diag_in[c].append(remote(block, block, beside))

    late = [[] for _ in far_shards]

    def head_share(copies, g, w):
        for e, shard in enumerate(far_shards):
            for c in range(CHUNKS):
                arrive(copies[c][e])
            at = pl.ds(pl.multiple_of((g * 2 + w % 2) * part, part), part)
            block = wh_v.at[shard, at]
            late[e].append(remote(block, block, sibling))

    y_in[0] = head_out(0)

    loads["x"].wait()
    normed_v[...] = normalize(x_v[...].astype(jnp.float32)).astype(jnp.bfloat16)
    loads["wk"].wait()
    loads["wv"].wait()
    kv_far, kv_near = [], []
    for p in range(PAIRS):
        kv_v[seq, p, :, :KP] = jnp.dot(
            normed_v[...], wk_v[:, p * KP : (p + 1) * KP], preferred_element_type=jnp.float32
        ).astype(jnp.bfloat16)
        kv_v[seq, p, :, KP:] = jnp.dot(
            normed_v[...], wv_v[:, p * VP : (p + 1) * VP], preferred_element_type=jnp.float32
        ).astype(jnp.bfloat16)
        block = kv_v.at[seq, p]
        kv_far.append([remote(block, block, dev(grp, win, s)) for s in peers])
        kv_near.append([remote(block, block, sibling)])
    for c in range(1, CHUNKS):
        y_in[c] = head_out(c)
    loads["wq"].wait()
    q_v[...] = jnp.dot(normed_v[...], wq_v[...], preferred_element_type=jnp.float32).astype(
        jnp.bfloat16
    )
    loads["skip"].wait()
    for j in range(width // 128):
        wide_v[j] = skip_v[:, j * 128 : (j + 1) * 128].astype(jnp.float32)

    def kv_relay(p):
        for e in range(half - 1):
            kv_far[p][e].wait_recv()
            block = kv_v.at[(seq + n - 2 * (e + 1)) % n, p]
            kv_near[p].append(remote(block, block, sibling))

    def attend(p):
        for copy in kv_near[p]:
            copy.wait_recv()
        keys = kv_v[:, p, :, :KP].reshape(n * tok, KP)
        vals = kv_v[:, p, :, KP:].reshape(n * tok, VP)
        pair = q_v[:, p * KP : (p + 1) * KP]
        key_lane = lax.broadcasted_iota(jnp.int32, (tok, KP), 1)
        outs = []
        for h in range(2):
            mine = key_lane < KEY if h == 0 else key_lane >= KEY
            masked = jnp.where(mine, pair.astype(jnp.float32), 0.0).astype(jnp.bfloat16)
            scores = lax.dot_general(
                masked, keys, (((1,), (1,)), ((), ())), preferred_element_type=jnp.float32
            ) * (1.0 / math.sqrt(KEY))
            expo = jnp.exp(scores - jnp.max(scores, axis=-1, keepdims=True))
            denom = jnp.sum(expo, axis=-1, keepdims=True)
            outs.append(
                jnp.dot(expo.astype(jnp.bfloat16), vals, preferred_element_type=jnp.float32) / denom
            )
        val_lane = lax.broadcasted_iota(jnp.int32, (tok, VP), 1)
        att_v[:, p * VP : (p + 1) * VP] = jnp.where(val_lane < VAL, outs[0], outs[1]).astype(
            jnp.bfloat16
        )

    kv_relay(0)
    head_spread(0)
    attend(0)
    for p in range(1, PAIRS):
        kv_relay(p)
        attend(p)
    head_spread(1)
    head_relay(0)
    own_sib = remote(wh_h, wh_v.at[seq], sibling)
    loads["wo"].wait()

    def up_step(t, carry):
        at = pl.ds(pl.multiple_of(t * TILE, TILE), TILE)
        resid = x_v[:, at].astype(jnp.float32) + jnp.dot(
            att_v[...], wo_v[:, at], preferred_element_type=jnp.float32
        )
        for m in range(2):
            here = pl.ds(pl.multiple_of(t * TILE + m * 128, 128), 128)
            mine = resid[:, m * 128 : (m + 1) * 128]
            even = (mine + wide_v[t * (TILE // 128) + m, pl.ds(0, tok, stride=2), :]).astype(jnp.bfloat16)
            odd = (mine + wide_v[t * (TILE // 128) + m, pl.ds(1, tok, stride=2), :]).astype(jnp.bfloat16)
            even = even.astype(jnp.float32)
            odd = odd.astype(jnp.float32)
            even_v[:, here] = even
            odd_v[:, here] = odd
            halo_s[0, :, here] = even[:8]
            halo_s[1, :, here] = odd[tok - 8 :]
        return carry

    lax.fori_loop(0, width // TILE, up_step, 0)
    to_prev = remote(halo_s.at[0], halo_r.at[0], dev(grp, win, (seq + n - 1) % n))
    to_next = remote(halo_s.at[1], halo_r.at[1], dev(grp, win, (seq + 1) % n))
    head_spread(2)
    loads["taps"].wait()
    to_prev.wait_recv()
    to_next.wait_recv()

    def conv_step(t, carry):
        at = pl.ds(pl.multiple_of(t * 128, 128), 128)
        even = even_v[:, at]
        odd = odd_v[:, at]
        row = lax.broadcasted_iota(jnp.int32, (tok, 128), 0)
        before = jnp.where(seq == 0, 0.0, halo_r[1, 7:8, at])
        after = jnp.where(seq == n - 1, 0.0, halo_r[0, 0:1, at])
        odd_prev = jnp.where(row == 0, before, pltpu.roll(odd, 1, axis=0))
        even_next = jnp.where(row == tok - 1, after, pltpu.roll(even, tok - 1, axis=0))
        t0, t1, t2 = taps_v[0:1, at], taps_v[1:2, at], taps_v[2:3, at]
        first = t0 * odd_prev + t1 * even + t2 * odd
        second = t0 * even + t1 * odd + t2 * even_next
        wide_v[t, pl.ds(0, tok, stride=2), :] = gelu(first)
        wide_v[t, pl.ds(1, tok, stride=2), :] = gelu(second)
        return carry

    band = width // BANDS
    lanes = band // 128
    feats = []
    for b in range(BANDS):
        lax.fori_loop(b * lanes, (b + 1) * lanes, conv_step, 0)
        for k in range(n):
            for j in range(b * lanes, (b + 1) * lanes):
                feat_v[k, :, j * 128 : (j + 1) * 128] = wide_v[
                    j, k * piece : (k + 1) * piece, :
                ].astype(jnp.bfloat16)
        span = pl.ds(b * band, band)
        for d in list(range(half, n)) + list(range(1, half)):
            owner = (seq + d) % n
            feats.append(
                pltpu.make_async_remote_copy(
                    src_ref=feat_v.at[owner, :, span],
                    dst_ref=mid_v.at[seq, :, span],
                    send_sem=fsend_sem.at[d, b],
                    recv_sem=frecv_sem.at[seq, b],
                    device_id=dev(grp, win, owner),
                    device_id_type=MESH,
                )
            )
            feats[-1].start()
        mid_v[seq, :, span] = feat_v[seq, :, span]
        if b == 1:
            head_spread(3)

    def feature_wait(slot, b):
        span = pl.ds(b * band, band)
        pltpu.make_async_remote_copy(
            src_ref=feat_v.at[slot, :, span],
            dst_ref=mid_v.at[slot, :, span],
            send_sem=fsend_sem.at[0, b],
            recv_sem=frecv_sem.at[slot, b],
            device_id=dev(grp, win, slot),
            device_id_type=MESH,
        ).wait_recv()

    behind = []

    def feature_forward(b):
        span = pl.ds(b * band, band)
        for i in range(half):
            at = (seq + i) % half
            if i == 0:

                @pl.when(seq < half)
                def _():
                    feature_wait(half + at, b)

            else:
                feature_wait(half + at, b)
            behind.append(
                pltpu.make_async_remote_copy(
                    src_ref=mid_v.at[half + at, :, span],
                    dst_ref=got_v.at[at, :, span],
                    send_sem=bsend_sem.at[i, b],
                    recv_sem=brecv_sem.at[i, b],
                    device_id=dev(grp, next_win, seq),
                    device_id_type=MESH,
                )
            )
            behind[-1].start()

    head_relay(1)
    head_relay(2)
    feature_forward(0)
    head_relay(3)
    feature_forward(1)
    for b in range(2, BANDS):
        feature_forward(b)
    head_share(y_in, grp, win)
    loads["wh"].wait()
    head_share(x_in, other_grp, win)
    head_share(z_in, grp, other_win)
    head_share(diag_in, other_grp, other_win)
    loads["bias"].wait()

    for i in range(half):
        at = (seq + i) % half
        for b in range(BANDS):
            if i == 0:

                @pl.when(seq >= half)
                def _():
                    feature_wait(at, b)

            else:
                feature_wait(at, b)
    for copy in behind:
        copy.wait_recv()

    def blend_step(t, carry):
        at = pl.ds(pl.multiple_of(t * 128, 128), 128)
        blocks = []
        for i in range(half):
            place = lax.broadcasted_iota(jnp.int32, (piece, 128), 0) + (i * n + seq) * piece
            place = place.astype(jnp.float32)
            blocks.append(
                (
                    (place + 1.0) * mid_v[i, :, at].astype(jnp.float32)
                    + (window_len - place) * got_v[i, :, at].astype(jnp.float32)
                )
                * (1.0 / (window_len + 1.0))
            )
        blend_v[:, at] = jnp.concatenate(blocks, axis=0).astype(jnp.bfloat16)
        return carry

    lax.fori_loop(0, width // 128, blend_step, 0)

    def apply_head(shard):
        def head_step(t, carry):
            at = pl.ds(pl.multiple_of(t * TILE, TILE), TILE)
            base = pl.ds(pl.multiple_of(shard * cols + t * TILE, TILE), TILE)
            z = (
                jnp.dot(blend_v[...], wh_v[shard, :, at], preferred_element_type=jnp.float32)
                + bias_v[:, base]
            )
            z = jnp.maximum(z, 0.0) + jnp.log1p(jnp.exp(-jnp.abs(z)))
            for i in range(half):
                out_v[i, :, base] = z[i * piece : (i + 1) * piece].astype(jnp.bfloat16)
            return carry

        lax.fori_loop(0, cols // TILE, head_step, 0)

    stores = []

    def store(shard):
        base = pl.ds(pl.multiple_of(shard * cols, cols), cols)
        at = len(stores)
        stores.append(
            pltpu.make_async_copy(out_v.at[:, :, base], out_h.at[:, :, base], store_sem.at[at])
        )
        stores[at].start()

    apply_head(seq)
    store(seq)
    own_sib.wait_recv()
    apply_head(sib_seq)
    store(sib_seq)
    for e in range(half - 1):
        shard = (seq + n - 2 * (e + 1)) % n
        apply_head(shard)
        store(shard)
    for e in range(half - 1):
        for copy in late[e]:
            copy.wait_recv()
        shard = (sib_seq + n - 2 * (e + 1)) % n
        apply_head(shard)
        store(shard)

    for copy in stores:
        copy.wait()
    for copy in started:
        copy.wait_send()
    for copy in feats + behind:
        copy.wait_send()


def local(embeddings, skip_rows, w_query, w_key, w_value, w_out, conv_taps, w_head, head_bias):
    n = lax.axis_size("seq")
    n_win = lax.axis_size("win")
    n_grp = lax.axis_size("grp")
    _, tok, width = embeddings.shape
    cols = w_head.shape[1]
    piece = 2 * tok // n
    half = n // 2
    others = half - 1
    copies = PAIRS * (2 * others + 1) + 1 + (4 * CHUNKS + 4) * others + 2
    bf16, f32 = jnp.bfloat16, jnp.float32
    dma = pltpu.SemaphoreType.DMA
    tracks = pl.pallas_call(
        functools.partial(kernel, n, n_win, n_grp),
        out_shape=jax.ShapeDtypeStruct((half, piece, n * cols), bf16),
        in_specs=[pl.BlockSpec(memory_space=pl.ANY)] * 9,
        out_specs=pl.BlockSpec(memory_space=pl.ANY),
        scratch_shapes=[
            pltpu.VMEM((tok, width), bf16),
            pltpu.VMEM((2 * tok, width), bf16),
            pltpu.VMEM(w_query.shape, bf16),
            pltpu.VMEM(w_key.shape, bf16),
            pltpu.VMEM(w_value.shape, bf16),
            pltpu.VMEM(w_out.shape, bf16),
            pltpu.VMEM(conv_taps.shape, f32),
            pltpu.VMEM((1, n * cols), f32),
            pltpu.VMEM((n, width, cols), bf16),
            pltpu.VMEM((tok, width), bf16),
            pltpu.VMEM((tok, HEADS * KEY), bf16),
            pltpu.VMEM((n, PAIRS, tok, KP + VP), bf16),
            pltpu.VMEM((tok, HEADS * VAL), bf16),
            pltpu.VMEM((width // 128, 2 * tok, 128), f32),
            pltpu.VMEM((tok, width), f32),
            pltpu.VMEM((tok, width), f32),
            pltpu.VMEM((2, 8, width), f32),
            pltpu.VMEM((2, 8, width), f32),
            pltpu.VMEM((n, piece, width), bf16),
            pltpu.VMEM((n, piece, width), bf16),
            pltpu.VMEM((half, piece, width), bf16),
            pltpu.VMEM((tok, width), bf16),
            pltpu.VMEM((half, piece, n * cols), bf16),
            dma((9,)),
            dma((copies,)),
            dma((copies,)),
            dma((n, BANDS)),
            dma((n, BANDS)),
            dma((half, BANDS)),
            dma((half, BANDS)),
            dma((n,)),
        ],
        compiler_params=pltpu.CompilerParams(
            collective_id=0, has_side_effects=True, vmem_limit_bytes=60 * 1024 * 1024
        ),
    )(
        embeddings, skip_rows, w_query, w_key, w_value, w_out, conv_taps, w_head,
        head_bias.reshape(1, -1),
    )
    return tracks[None, :, None]


def solution(mesh):
    return jax.shard_map(
        local,
        mesh=mesh,
        in_specs=(
            P(("grp", "win"), "seq", None),
            P(("grp", "win"), "seq", None),
            P(),
            P(),
            P(),
            P(),
            P(),
            P(None, "seq"),
            P(),
        ),
        out_specs=P(("grp", "win"), None, "seq", None, None),
        check_vma=False,
    )
```
